32 devices in a mesh: dp: 16 (over z, y, core), seq: 2 (over x).
Axes of the slice: x: 2, y: 2, z: 4, core: 2. Of those that a mesh axis runs over, the one named last changes fastest.
Arguments:
- hidden_in: bfloat16 [4096, 2048], P(('dp', 'seq')), may hold values from -6 to 6
- norm_gain: float32 [2048], replicated, may hold values from 0.5 to 1.5
- resid_grad: bfloat16 [4096, 2048], P(('dp', 'seq')), may hold values from -3 to 3
- key_output_gradient: bfloat16 [4096, 512], P('dp', 'seq'), may hold values from -6 to 6
- value_output_gradient: bfloat16 [4096, 512], P('dp', 'seq'), may hold values from -6 to 6
- key_matrix: bfloat16 [2048, 512], P(None, 'seq'), may hold values from -0.125 to 0.125
- value_matrix: bfloat16 [2048, 512], P(None, 'seq'), may hold values from -0.125 to 0.125
Outputs:
- input_grad: bfloat16 [4096, 2048], P(('dp', 'seq'))
- key_weight_grad: float32 [2048, 512], P('dp', 'seq')
- value_weight_grad: float32 [2048, 512], P('dp', 'seq')
- gain_grad: float32 [2048], replicated
The draws below stay inside these ranges and needn't reach their ends.
All inputs are finite; a program needn't handle non-finite values.
Results may differ from the reference program's by a relative error of at most 0.0029.
Values may be sent and summed in bfloat16 or wider, within the bound.
No kernel may reach another device: no remote copies, remote signals or barrier semaphores. Data moves between devices by JAX's collectives and lax.ppermute only.
A program may use at most 64 MiB of HBM per device.

```python
import math
import jax
import jax.numpy as jnp
from jax import lax

MODEL_DIMENSION = 2048
KEY_VALUE_HEADS = 4
HEAD_SIZE = 128
TOKEN_COUNT = 4096


def block_scale(rng, extent, cuts, smallest, top_value):
    def one(axis_at, blocks):
        draws = jax.random.uniform(jax.random.fold_in(jax.random.fold_in(rng, 6), axis_at), (blocks,), jnp.float32, smallest / len(cuts), top_value / len(cuts))
        return jnp.repeat(jnp.exp(draws), extent[axis_at] // blocks).reshape((-1,) + (1,) * (len(extent) - axis_at - 1))

    level = one(*cuts[0])
    for cut in cuts[1:]:
        level = level * one(*cut)
    return level


def noise(key, extent, width, bound, split=(), held_as=jnp.bfloat16):
    drawn = jax.random.normal(key, extent, jnp.float32) * width
    if len(split) > 0:
        drawn = block_scale(key, extent, split, -0.22, 0.18) * drawn
    return jnp.clip(drawn, min=-bound, max=bound).astype(held_as)


def setup_inputs(seed: int = 0) -> dict:
    streams_of = jax.random.split(jax.random.key(seed), 8)
    return {
        "hidden_in": noise(streams_of[0], (TOKEN_COUNT, MODEL_DIMENSION), 1.0, 6.0, ((0, 32),)),
        "norm_gain": jnp.clip(1.0 + 0.1 * jax.random.normal(streams_of[1], (MODEL_DIMENSION,), jnp.float32), 0.5, 1.5),
        "resid_grad": noise(streams_of[2], (TOKEN_COUNT, MODEL_DIMENSION), 0.5, 3.0, ((0, 32),)),
        "key_output_gradient": noise(streams_of[3], (TOKEN_COUNT, KEY_VALUE_HEADS * HEAD_SIZE), 1.0, 6.0, ((0, 16), (1, 2))),
        "value_output_gradient": noise(streams_of[4], (TOKEN_COUNT, KEY_VALUE_HEADS * HEAD_SIZE), 1.0, 6.0, ((0, 16), (1, 2))),
        "key_matrix": noise(streams_of[5], (MODEL_DIMENSION, KEY_VALUE_HEADS * HEAD_SIZE), MODEL_DIMENSION ** -0.5, 0.125, ((1, 2),)),
        "value_matrix": noise(streams_of[6], (MODEL_DIMENSION, KEY_VALUE_HEADS * HEAD_SIZE), MODEL_DIMENSION ** -0.5, 0.125, ((1, 2),)),
    }


def reference(hidden_in, norm_gain, resid_grad, key_output_gradient, value_output_gradient, key_matrix, value_matrix):
    scale = 1.0 / math.sqrt(TOKEN_COUNT)
    widened = hidden_in.astype(jnp.float32)
    inv_rms = lax.rsqrt(lax.optimization_barrier(jnp.mean(widened * widened, axis=-1, keepdims=True)) + 1e-05)
    unit_rows = widened * inv_rms
    normed = (unit_rows * norm_gain).astype(jnp.bfloat16)
    key_weight_grad = jnp.dot(normed.T, key_output_gradient, preferred_element_type=jnp.float32) * scale
    value_weight_grad = jnp.dot(normed.T, value_output_gradient, preferred_element_type=jnp.float32) * scale
    normed_grad = jnp.dot(key_output_gradient, key_matrix.T, preferred_element_type=jnp.float32)
    normed_grad = normed_grad + jnp.dot(value_output_gradient, value_matrix.T, preferred_element_type=jnp.float32)
    gain_grad = lax.optimization_barrier(jnp.sum(normed_grad * unit_rows, axis=0)) * scale
    scaled = normed_grad * norm_gain
    inner = lax.optimization_barrier(jnp.mean(scaled * unit_rows, axis=-1, keepdims=True))
    input_grad = (resid_grad.astype(jnp.float32) + inv_rms * (scaled - unit_rows * inner)).astype(jnp.bfloat16)
    return (input_grad, key_weight_grad, value_weight_grad, gain_grad)
```

```python
import functools
import math

import jax
import jax.numpy as jnp
from jax import lax
from jax.experimental import pallas as pl
from jax.experimental.pallas import tpu as pltpu
from jax.sharding import PartitionSpec as P

EPSILON = 1e-05
AXES = ("dp", "seq")
VMEM = pl.BlockSpec(memory_space=pltpu.VMEM)
F32, BF16 = jnp.float32, jnp.bfloat16


def exchange(value, mask, count):
    return lax.ppermute(value, AXES, [(i, i ^ mask) for i in range(count)])


def place(tokens_split):
    dp = lax.axis_index("dp")
    return dp // 2, lax.rem(dp, 2), lax.axis_index("seq")


def mirrored(position, bits):
    return sum(((position >> i) & 1) << (bits - 1 - i) for i in range(bits))


def unit_of(hidden):
    widened = hidden.astype(F32)
    inv_rms = lax.rsqrt(jnp.mean(widened * widened, axis=-1, keepdims=True) + EPSILON)
    return inv_rms, widened * inv_rms


def norm_kernel(chips, hidden_ref, gain_ref, *refs):
    *outs, turned = refs
    other_all, mine, other = outs[0], outs[1:5], outs[5:9]
    chip, core, _ = place(None)
    bits = chips.bit_length() - 1
    rows = hidden_ref.shape[1] // (2 * chips)
    _, unit = unit_of(hidden_ref[...])
    turned[...] = (unit * gain_ref[...]).astype(BF16).T
    per = chips // 4
    for position in range(chips):
        group, at = position // per, position % per
        block = (mirrored(position, bits) ^ chip) * 2
        for side, dest in ((core, mine), (1 - core, other)):
            start = pl.multiple_of((block + side) * rows, rows)
            piece = turned[pl.ds(start, rows), :]
            dest[group][at * rows : (at + 1) * rows, :] = piece
            if dest is other:
                other_all[position * rows : (position + 1) * rows, :] = piece


def normalize(hidden, gain, chips):
    tokens, width = hidden.shape
    quarter = jax.ShapeDtypeStruct((width // 8, tokens), BF16)
    out = [jax.ShapeDtypeStruct((width // 2, tokens), BF16)] + [quarter] * 8
    outs = pl.pallas_call(
        functools.partial(norm_kernel, chips),
        out_shape=out,
        in_specs=[VMEM] * 2,
        out_specs=[VMEM] * 9,
        scratch_shapes=[pltpu.VMEM((width, tokens), BF16)],
        cost_estimate=pl.CostEstimate(flops=5 * tokens * width, bytes_accessed=6 * tokens * width, transcendentals=tokens),
        name="norm",
    )(hidden, gain)
    return outs[0], outs[1:5], outs[5:9]


def partial_kernel(splits, key_grad_ref, value_grad_ref, key_ref, value_ref, *outs):
    _, _, at = place(None)
    tokens = key_grad_ref.shape[0] // splits
    contract = (((1,), (1,)), ((), ()))
    for r in range(splits - 1, -1, -1):
        start = pl.multiple_of((at ^ r) * tokens, tokens)
        part = lax.dot_general(
            key_grad_ref[pl.ds(start, tokens), :], key_ref[...], contract, preferred_element_type=F32
        ) + lax.dot_general(
            value_grad_ref[pl.ds(start, tokens), :], value_ref[...], contract, preferred_element_type=F32
        )
        outs[r][...] = part.astype(outs[r].dtype)


def partial_products(key_grad, value_grad, key_matrix, value_matrix, splits):
    total, columns = key_grad.shape
    width = key_matrix.shape[0]
    tokens = total // splits
    step = width // 4
    whole = pl.BlockSpec((total, columns), lambda i: (0, 0))
    matrix = pl.BlockSpec((step, columns), lambda i: (i, 0))
    return pl.pallas_call(
        functools.partial(partial_kernel, splits),
        grid=(width // step,),
        out_shape=[jax.ShapeDtypeStruct((tokens, width), F32)]
        + [jax.ShapeDtypeStruct((tokens, width), BF16)] * (splits - 1),
        in_specs=[whole, whole, matrix, matrix],
        out_specs=[pl.BlockSpec((tokens, step), lambda i: (0, i))] * splits,
        cost_estimate=pl.CostEstimate(
            flops=4 * total * columns * width,
            bytes_accessed=4 * (total + width) * columns + 4 * total * width,
            transcendentals=0,
        ),
        name="partial",
    )(key_grad, value_grad, key_matrix, value_matrix)


def weight_kernel(splits, plan, groups, sources, *refs):
    blocks, refs = refs[: groups * 2 * splits], refs[groups * 2 * splits :]
    grads, outs = refs[: 2 * sources], refs[2 * sources :]
    _, _, at = place(None)
    tokens = blocks[0].shape[1]
    starts = [pl.multiple_of((at ^ r) * tokens, tokens) for r in range(splits)]
    right = [
        jnp.concatenate(
            [grads[2 * source + side][pl.ds(start, tokens), :] for side in (0, 1) for start in starts], axis=0
        )
        for source in range(sources)
    ]
    left = [
        jnp.concatenate([b[...] for b in blocks[g * 2 * splits : (g + 1) * 2 * splits]], axis=1)
        for g in range(groups)
    ]
    for (wanted, source), out in zip(plan, outs):
        height = left[0].shape[0]
        for i, g in enumerate(wanted):
            out[i * height : (i + 1) * height, :] = jnp.dot(
                left[g], right[source], preferred_element_type=F32
            ).astype(out.dtype)


def weight_products(blocks, grads, plan, dtype, splits, name):
    height, tokens = blocks[0][0].shape
    columns = grads[0][0].shape[1]
    flat = [b for group in blocks for b in group] + [g for pair in grads for g in pair]
    outs = [jax.ShapeDtypeStruct((len(wanted) * height, columns), dtype) for wanted, _ in plan]
    rows = sum(o.shape[0] for o in outs)
    return pl.pallas_call(
        functools.partial(weight_kernel, splits, plan, len(blocks), len(grads)),
        out_shape=outs,
        in_specs=[VMEM] * len(flat),
        out_specs=[VMEM] * len(outs),
        cost_estimate=pl.CostEstimate(
            flops=2 * rows * columns * 2 * splits * tokens,
            bytes_accessed=sum(a.size * a.dtype.itemsize for a in flat) + 4 * rows * columns,
            transcendentals=0,
        ),
        name=name,
    )(*flat)


def input_kernel(hidden_ref, gain_ref, resid_ref, own_ref, *refs):
    *parts, out_ref, sum_ref = refs
    grad = own_ref[...]
    for part in parts:
        grad = grad + part[...].astype(F32)
    inv_rms, unit = unit_of(hidden_ref[...])
    sums = jnp.sum(grad * unit, axis=0, keepdims=True)

    @pl.when(pl.program_id(0) == 0)
    def _():
        sum_ref[...] = sums

    @pl.when(pl.program_id(0) > 0)
    def _():
        sum_ref[...] += sums

    scaled = grad * gain_ref[...]
    inner = jnp.mean(scaled * unit, axis=-1, keepdims=True)
    out_ref[...] = (resid_ref[...].astype(F32) + inv_rms * (scaled - unit * inner)).astype(BF16)


def input_gradient(hidden, gain, resid, own, parts):
    tokens, width = hidden.shape
    step = tokens // 4
    block = pl.BlockSpec((step, width), lambda i: (i, 0))
    row = pl.BlockSpec((1, width), lambda i: (0, 0))
    return pl.pallas_call(
        input_kernel,
        grid=(tokens // step,),
        out_shape=[jax.ShapeDtypeStruct((tokens, width), BF16), jax.ShapeDtypeStruct((1, width), F32)],
        in_specs=[block, row, block, block] + [block] * len(parts),
        out_specs=[block, row],
        cost_estimate=pl.CostEstimate(
            flops=20 * tokens * width, bytes_accessed=12 * tokens * width, transcendentals=tokens
        ),
        name="input",
    )(hidden, gain, resid, own, *parts)


def per_device(
    splits,
    chips,
    hidden_in,
    norm_gain,
    resid_grad,
    key_output_gradient,
    value_output_gradient,
    key_matrix,
    value_matrix,
):
    width = hidden_in.shape[1]
    count = 2 * chips * splits
    core_mask, chip_mask = splits, 2 * splits
    scale = 1.0 / math.sqrt(key_output_gradient.shape[0] * 2 * chips)
    gain = norm_gain.reshape(1, width)
    swap = functools.partial(exchange, count=count)

    other_all, mine, other = normalize(hidden_in, gain, chips)
    key_pair = (key_output_gradient, swap(key_output_gradient, core_mask))
    value_pair = (value_output_gradient, swap(value_output_gradient, core_mask))
    sibling = swap(other_all, core_mask)
    quarter = sibling.shape[0] // 4
    blocks = [None] * 4
    for g in (3, 2, 1, 0):
        blocks[g] = (
            [mine[g]]
            + [swap(mine[g], r) for r in range(1, splits)]
            + [sibling[g * quarter : (g + 1) * quarter]]
            + [swap(other[g], core_mask + r) for r in range(1, splits)]
        )
    own, *sends = partial_products(
        key_output_gradient, value_output_gradient, key_matrix, value_matrix, splits
    )
    parts = [swap(send, r + 1) for r, send in enumerate(sends)]

    (key_send,) = weight_products(
        [blocks[2], blocks[3]], [key_pair], (((0, 1), 0),), BF16, splits, "key_send"
    )
    key_got = swap(key_send, chip_mask)
    (value_send,) = weight_products(
        [blocks[1], blocks[3]], [value_pair], (((0, 1), 0),), BF16, splits, "value_send"
    )
    value_got = swap(value_send, 2 * chip_mask)
    key_keep, value_keep = weight_products(
        [blocks[0], blocks[1], blocks[2]],
        [key_pair, value_pair],
        (((0, 1), 0), ((0, 2), 1)),
        F32,
        splits,
        "keep",
    )
    bits = chips.bit_length() - 1
    for step in range(1, bits):
        half = key_keep.shape[0] // 2
        key_bit = step
        value_bit = 0 if step == 1 else step
        key_sum = key_keep + key_got.astype(F32)
        value_sum = value_keep + value_got.astype(F32)
        key_got = swap(key_sum[half:].astype(BF16), chip_mask << key_bit)
        value_got = swap(value_sum[half:].astype(BF16), chip_mask << value_bit)
        key_keep, value_keep = key_sum[:half], value_sum[:half]
    key_total = (key_keep + key_got.astype(F32)) * scale
    value_total = (value_keep + value_got.astype(F32)) * scale

    input_grad, gain_sum = input_gradient(hidden_in, gain, resid_grad, own, parts)
    mask = core_mask
    masks = [core_mask] + [chip_mask << b for b in range(bits)]
    masks += [1 << b for b in range(splits.bit_length() - 1)]
    gain_sum = gain_sum.reshape(8, width // 8)
    for mask in masks:
        gain_sum = gain_sum + swap(gain_sum, mask)
    return (input_grad, key_total, value_total, gain_sum.reshape(width) * scale)


def solution(mesh):
    splits, chips = mesh.shape["seq"], mesh.shape["dp"] // 2
    return jax.shard_map(
        functools.partial(per_device, splits, chips),
        mesh=mesh,
        in_specs=(
            P(("dp", "seq"), None),
            P(),
            P(("dp", "seq"), None),
            P("dp", "seq"),
            P("dp", "seq"),
            P(None, "seq"),
            P(None, "seq"),
        ),
        out_specs=(P(("dp", "seq"), None), P("dp", "seq"), P("dp", "seq"), P()),
        check_vma=False,
    )
```
